32 devices in a mesh: section: 2 (over x), shard: 8 (over z, y), rep: 2 (over core).
Axes of the slice: x: 2, y: 2, z: 4, core: 2. Of those that a mesh axis runs over, the one named last changes fastest.
Arguments:
- boundary_in: bfloat16 [2, 16384, 1024], P('section', ('shard', 'rep')), may hold values from -6 to 6
- segment_ids: int32 [32, 512], P(('shard', 'rep')), may hold values from 0 to 7, never falling along the last dimension, each value on 1 to 200 neighbouring positions
- keep_mask: int32 [32, 512], P(('shard', 'rep')), may hold values 0 or 1
- w_qkv: bfloat16 [2, 1024, 3072], P('section', 'shard'), may hold values from -0.1875 to 0.1875
- w_out: bfloat16 [2, 1024, 1024], P('section', 'shard'), may hold values from -0.5 to 0.5
- w_up: bfloat16 [2, 1024, 4096], P('section', 'shard'), may hold values from -0.1875 to 0.1875
- w_down: bfloat16 [2, 4096, 1024], P('section', 'shard'), may hold values from -0.09375 to 0.09375
- norm_gains: bfloat16 [2, 2, 1024], P('section', None, 'shard'), may hold values from 0.5 to 1.5
- biases: bfloat16 [2, 6, 1024], P('section', None, 'shard'), may hold values from -3 to 3
- up_bias: bfloat16 [2, 4096], P('section', 'shard'), may hold values from -3 to 3
Outputs:
- boundary_out: bfloat16 [2, 16384, 1024], P('section', ('shard', 'rep'))
- grad_qkv: float32 [2, 1024, 3072], P('section', 'shard')
- grad_out: float32 [2, 1024, 1024], P('section', 'shard')
- grad_up: float32 [2, 1024, 4096], P('section', 'shard')
- grad_down: float32 [2, 4096, 1024], P('section', 'shard')
- grad_gains: float32 [2, 2, 1024], P('section', None, 'shard')
- grad_biases: float32 [2, 6, 1024], P('section', None, 'shard')
- grad_up_bias: float32 [2, 4096], P('section', 'shard')
The draws below stay inside these ranges and needn't reach their ends.
Inputs may be any that keep to these rules, and one draw needn't show every extreme that they name: `segment_ids`: in each sequence the ids rise by one from document to document, a document has 1 to 200 tokens.
All inputs are finite; a program needn't handle non-finite values. No bound on the sum of `keep_mask` on one device may be relied on, other than what follows from the above.
Results may differ from the reference program's by a relative error of at most 0.019.
Values may be sent and summed in bfloat16 or wider, within the bound.
No kernel may reach another device: no remote copies, remote signals or barrier semaphores. Data moves between devices by JAX's collectives and lax.ppermute only.
A program may use at most 320 MiB of HBM per device.

```python
import math
import jax
import jax.numpy as jnp
import numpy as np
from jax import lax

D = 1024
HEAD = 64
FF = 4096
SEQ_LEN = 512
SEG_COUNT = 8
SEG_MOST = 200
SEQS = 32
TOKENS = 16384


def plant(values, key, least, high):
    extent = values.shape
    index_at = [jax.random.randint(jax.random.fold_in(key, axis), (), 0, extent[axis]) for axis in range(len(extent))]
    values = values.at[tuple(index_at)].set(least)
    longest = extent.index(max(extent))
    index_at[longest] = (index_at[longest] + 1) % extent[longest]
    return values.at[tuple(index_at)].set(high)


def steps_of(rng, dims, shards, smallest, largest):
    loudness = 1.0
    for axis_at, shards_of in shards:
        draws = jax.random.uniform(jax.random.fold_in(jax.random.fold_in(rng, 6), axis_at), (shards_of,), jnp.float32, smallest / len(shards), largest / len(shards))
        loudness = loudness * jnp.repeat(jnp.exp(draws), dims[axis_at] // shards_of).reshape((-1,) + (1,) * (len(dims) - 1 - axis_at))
    return loudness


def split_up(amount, total, reach, skew):
    weights = [(1 << 20) // math.isqrt(standing ** skew) + 1 for standing in range(2, amount + 1)]
    spare, counts = total - reach - (amount - 1), [1] * (amount - 1)
    while spare > 0:
        free = [i for i in range(amount - 1) if counts[i] < reach]
        pool, left = sum([weights[i] for i in free]), spare
        for i in free:
            addition = min(reach - counts[i], max(1, left * weights[i] // pool), spare)
            counts[i] = counts[i] + addition
            spare = spare - addition
    return np.array([reach] + counts)


def uneven(stream_key, amount, total, most, lean):
    if amount == 2:
        one = jax.random.randint(stream_key, (), max(1, total - most), min(most, total - 1) + 1)
        return jnp.stack([one, total - one])
    tallies = jnp.asarray(split_up(amount, total, most, lean), jnp.int32)
    couples = (amount - 1) // 2
    giver, receiver = tallies[1:1 + 2 * couples:2], tallies[2:2 + 2 * couples:2]
    slack = jnp.minimum(giver - 1, most - receiver)
    moved = jax.random.randint(jax.random.fold_in(stream_key, 1), (couples,), 0, 1 << 20) % (slack + 1)
    tallies = tallies.at[1:1 + 2 * couples:2].set(giver - moved).at[2:2 + 2 * couples:2].set(receiver + moved)
    return tallies[jax.random.permutation(jax.random.fold_in(stream_key, 2), amount)]


def gaussian(stream_key, dims, scale, reach, cuts=(), kind=jnp.bfloat16):
    factor_of = steps_of(stream_key, dims, cuts, -0.22, 0.18) if cuts else 1.0
    entries = jax.random.normal(stream_key, dims, jnp.float32) * scale * factor_of
    return jnp.minimum(jnp.maximum(entries, -reach), reach).astype(kind)


def setup_inputs(seed: int = 0) -> dict:
    streams_of = jax.random.split(jax.random.key(seed), 11)
    return {
        "boundary_in": gaussian(streams_of[0], (2, TOKENS, D), 1.0, 6.0, ((0, 2), (1, 16))),
        "segment_ids": jax.vmap(lambda own: jnp.searchsorted(jnp.cumsum(uneven(own, SEG_COUNT, SEQ_LEN, SEG_MOST, 0)), jnp.arange(SEQ_LEN), side="right"))(jax.random.split(streams_of[1], SEQS)).reshape((SEQS, SEQ_LEN)).astype(jnp.int32),
        "keep_mask": plant((jax.random.randint(streams_of[2], (SEQS, SEQ_LEN), 0, 8) < 7).astype(jnp.int32), jax.random.fold_in(streams_of[2], 1), 0, 1),
        "w_qkv": gaussian(streams_of[3], (2, D, 3 * D), D ** -0.5, 0.1875, ((0, 2), (1, 8))),
        "w_out": gaussian(streams_of[4], (2, D, D), (D // 8) ** -0.5, 0.5, ((0, 2), (1, 8))),
        "w_up": gaussian(streams_of[5], (2, D, FF), D ** -0.5, 0.1875, ((0, 2), (1, 8))),
        "w_down": gaussian(streams_of[6], (2, FF, D), FF ** -0.5, 0.09375, ((0, 2), (1, 8))),
        "norm_gains": jnp.clip(1.0 + 0.1 * jax.random.normal(streams_of[7], (2, 2, D), jnp.float32), 0.5, 1.5).astype(jnp.bfloat16),
        "biases": gaussian(streams_of[8], (2, 6, D), 0.3, 3.0, ((0, 2), (2, 8))),
        "up_bias": gaussian(streams_of[9], (2, FF), 0.5, 3.0, ((0, 2), (1, 8))),
    }


@jax.custom_vjp
def low(v):
    return lax.optimization_barrier(v.astype(jnp.bfloat16)).astype(jnp.float32)

@jax.custom_vjp
def low_back(v):
    return v

def low_keep(v):
    return (low(v), None)

def low_pass(kept, grad):
    return (grad,)

def back_keep(v):
    return (v, None)

def back_low(kept, grad):
    return (low(grad),)
low.defvjp(low_keep, low_pass)
low_back.defvjp(back_keep, back_low)
epsilon = 1e-12

def normalize(rows_in, gain, shift):
    centre = lax.optimization_barrier(jnp.mean(rows_in, axis=-1, keepdims=True))
    centered = rows_in - centre
    variance = lax.optimization_barrier(jnp.mean(centered * centered, axis=-1, keepdims=True))
    return centered * lax.rsqrt(variance + epsilon) * gain + shift

def gelu_exact(values):
    return 0.5 * values * (1.0 + lax.erf(values * 0.7071067811865476))

def matmul(left, right):
    return jnp.dot(left, right, precision=lax.Precision.HIGHEST, preferred_element_type=jnp.float32)

def attend_block(queries, keys_rows, values_rows, allowed):
    scores = jnp.einsum('qhe,khe->hqk', queries, keys_rows, precision=lax.Precision.HIGHEST)
    scores = low_back(scores * HEAD ** (-0.5))
    scores = jnp.where(allowed[None], scores, -1e+30)
    soft_rows = low(jax.nn.softmax(scores, axis=-1))
    return jnp.einsum('hqk,khe->qhe', soft_rows, values_rows, precision=lax.Precision.HIGHEST)

def layer(inputs, allowed, params):
    w_qkv, w_out, w_up, w_down, norm_gains, biases, up_bias = params
    width = w_out.shape[0]
    row_count = inputs.shape[0]
    seq_total = allowed.shape[0]
    joint = matmul(inputs, w_qkv)
    queries = low(low_back(joint[:, :width] + biases[0]))
    keys_rows = low(low_back(joint[:, width:2 * width]))
    values_rows = low(low_back(joint[:, 2 * width:] + biases[1]))
    head_shape = (seq_total, row_count // seq_total, width // HEAD, HEAD)
    checked_block = jax.checkpoint(attend_block)

    def one_sequence(packed):
        return checked_block(packed[0], packed[1], packed[2], packed[3])
    context = lax.map(one_sequence, (queries.reshape(head_shape), keys_rows.reshape(head_shape), values_rows.reshape(head_shape), allowed))
    context = low(low_back(context.reshape(row_count, width)))
    mixed = inputs + low_back(matmul(context, w_out) + biases[2])
    hidden = low(normalize(mixed, norm_gains[0], biases[3]))
    upper = low_back(matmul(hidden, w_up) + up_bias)
    activated = low(gelu_exact(upper))
    summed = hidden + low_back(matmul(activated, w_down) + biases[4])
    return normalize(summed, norm_gains[1], biases[5])

def reference(boundary_in, segment_ids, keep_mask, w_qkv, w_out, w_up, w_down, norm_gains, biases, up_bias):
    group = math.gcd(SEQS, max(1, 4096 // SEQ_LEN))
    group_count = SEQS // group
    stacks = tuple((item.astype(jnp.float32) for item in (w_qkv, w_out, w_up, w_down, norm_gains, biases, up_bias)))
    first_params = tuple((item[0] for item in stacks))
    second_params = tuple((item[1] for item in stacks))
    inputs = boundary_in[0].astype(jnp.float32).reshape(group_count, group * SEQ_LEN, D)
    cotangent = boundary_in[1].astype(jnp.float32).reshape(group_count, group * SEQ_LEN, D)
    seg_groups = segment_ids.reshape(group_count, group, SEQ_LEN)
    keep_groups = keep_mask.reshape(group_count, group, SEQ_LEN)

    def one_group(totals, pieces):
        rows_in, cot_rows, seg_rows, keep_rows = pieces
        allowed = (seg_rows[:, :, None] == seg_rows[:, None, :]) & (keep_rows[:, :, None] == keep_rows[:, None, :])

        def forward(first_in, first, second):
            middle = layer(first_in, allowed, first)
            return layer(low(low_back(middle)), allowed, second)
        result, back = jax.vjp(forward, rows_in, first_params, second_params)
        grad_in, grad_first, grad_second = back(cot_rows)
        totals = jax.tree.map(jnp.add, totals, (grad_first, grad_second))
        return (totals, (result.astype(jnp.bfloat16), grad_in.astype(jnp.bfloat16)))
    zeros = jax.tree.map(jnp.zeros_like, (first_params, second_params))
    totals, outputs = lax.scan(one_group, zeros, (inputs, cotangent, seg_groups, keep_groups))
    results, grads_in = outputs
    boundary_out = jnp.stack([grads_in.reshape(TOKENS, D), results.reshape(TOKENS, D)])
    first_totals, second_totals = totals
    stacked = tuple((jnp.stack([first_totals[place], second_totals[place]]) for place in range(7)))
    return (boundary_out, stacked[0], stacked[1], stacked[2], stacked[3], stacked[4], stacked[5], stacked[6])
```

```python
import functools

import jax
import jax.numpy as jnp
from jax import lax
from jax.experimental import pallas as pl
from jax.experimental.pallas import tpu as pltpu
from jax.sharding import PartitionSpec as P

HEAD = 64
MICRO = 2
PAIR = 2 * HEAD
CODES = 16
FF_BLOCKS = 4
LONGEST_RING = 16

epsilon = 1e-12
masked_score = -1e30
scale_head = HEAD ** (-0.5)


f32 = jnp.float32
bf16 = jnp.bfloat16


def matmul(left, right):
    return jnp.dot(left, right, preferred_element_type=f32)


def matmul_t(left, right):
    return lax.dot_general(left, right, (((1,), (1,)), ((), ())), preferred_element_type=f32)


def tmatmul(left, right):
    return lax.dot_general(left, right, (((0,), (0,)), ((), ())), preferred_element_type=f32)


def lanes_of(rows):
    return lax.broadcasted_iota(jnp.int32, (rows, PAIR), 1)


def attend_kernel(q_ref, k_ref, v_ref, hot_ref, bar_ref, context_ref, total_ref):
    rows = q_ref.shape[0]
    lane = lanes_of(rows)
    queries = q_ref[...] * scale_head
    keys_rows = k_ref[...]
    values_rows = v_ref[...]
    hot = hot_ref[...]
    bar = bar_ref[...]
    ones = jnp.ones_like(values_rows)
    contexts = []
    totals = []
    for head in range(2):
        own = (lane < HEAD) if head == 0 else (lane >= HEAD)
        scores = matmul_t(jnp.where(own, queries, hot), jnp.where(own, keys_rows, bar))
        top = jnp.max(scores, axis=1, keepdims=True)
        exponent = jnp.exp(scores - top).astype(bf16)
        both = matmul(exponent, jnp.where(own, values_rows, ones))
        row_total = pltpu.roll(both, HEAD, 1)
        contexts.append(both / row_total)
        totals.append(top + jnp.log(row_total))
    first = lane < HEAD
    context_ref[...] = jnp.where(first, contexts[0], contexts[1]).astype(bf16)
    total_ref[...] = jnp.where(first, totals[0], totals[1])


def attend(joint, hot, bar):
    rows, width = joint.shape[0], joint.shape[1] // 3
    pairs = width // PAIR
    block = lambda shift: pl.BlockSpec((rows, PAIR), lambda i: (0, shift + i))
    fixed = pl.BlockSpec((rows, PAIR), lambda i: (0, 0))
    return pl.pallas_call(
        attend_kernel,
        grid=(pairs,),
        in_specs=[block(0), block(pairs), block(2 * pairs), fixed, fixed],
        out_specs=[block(0), block(0)],
        out_shape=(
            jax.ShapeDtypeStruct((rows, width), bf16),
            jax.ShapeDtypeStruct((rows, width), f32),
        ),
        cost_estimate=pl.CostEstimate(
            flops=16 * rows * rows * width,
            bytes_accessed=12 * rows * width,
            transcendentals=2 * pairs * rows * rows,
        ),
        name="attend",
    )(joint, joint, joint, hot, bar)


def split_two(values):
    high = values.astype(bf16)
    return high, (values - high.astype(f32)).astype(bf16)


def attend_back_kernel(
    q_ref, k_ref, v_ref, hot_ref, bar_ref, total_ref, context_ref, grad_ref, out_ref
):
    rows = q_ref.shape[0]
    lane = lanes_of(rows)
    first = lane < HEAD
    queries = q_ref[...] * scale_head
    keys_rows = k_ref[...]
    values_rows = v_ref[...]
    grads = grad_ref[...]
    hot = hot_ref[...]
    bar = bar_ref[...]
    total_high, total_low = split_two(pltpu.roll(total_ref[...], HEAD, 1))
    product = grads.astype(f32) * context_ref[...].astype(f32)
    outs = []
    for head in range(2):
        own = first if head == 0 else jnp.logical_not(first)
        base = HEAD if head == 0 else 0
        high_lane = lane == base + CODES
        low_lane = lane == base + CODES + 1
        extra = jnp.where(high_lane, total_high, jnp.where(low_lane, total_low, hot))
        row_sum = jnp.sum(jnp.where(own, product, 0.0), axis=1, keepdims=True)
        sum_high, sum_low = split_two(jnp.broadcast_to(row_sum, product.shape))
        zeros = jnp.zeros_like(grads)
        grad_extra = jnp.where(high_lane, sum_high, jnp.where(low_lane, sum_low, zeros))
        minus = jnp.where(jnp.logical_or(high_lane, low_lane), -jnp.ones_like(grads), zeros)
        key_extra = jnp.where(jnp.logical_or(high_lane, low_lane), minus, bar)
        scores = matmul_t(jnp.where(own, keys_rows, key_extra), jnp.where(own, queries, extra))
        soft = jnp.exp(scores)
        grad_soft = matmul_t(
            jnp.where(own, values_rows, minus), jnp.where(own, grads, grad_extra)
        )
        grad_scores = (soft * grad_soft).astype(bf16)
        grad_values = matmul(soft.astype(bf16), grads)
        grad_keys = matmul(grad_scores, queries)
        grad_queries = tmatmul(grad_scores, keys_rows) * scale_head
        outs.append((grad_queries, grad_keys, grad_values))
    for place in range(3):
        out_ref[place] = jnp.where(first, outs[0][place], outs[1][place]).astype(bf16)


def attend_back(joint, hot, bar, total, context, grad_context):
    rows, width = context.shape
    pairs = width // PAIR
    block = lambda shift: pl.BlockSpec((rows, PAIR), lambda i: (0, shift + i))
    fixed = pl.BlockSpec((rows, PAIR), lambda i: (0, 0))
    return pl.pallas_call(
        attend_back_kernel,
        grid=(pairs,),
        in_specs=[block(0), block(pairs), block(2 * pairs), fixed, fixed]
        + [block(0), block(0), block(0)],
        out_specs=pl.BlockSpec((3, rows, PAIR), lambda i: (0, 0, i)),
        out_shape=jax.ShapeDtypeStruct((3, rows, width), bf16),
        cost_estimate=pl.CostEstimate(
            flops=40 * rows * rows * width,
            bytes_accessed=20 * rows * width,
            transcendentals=2 * pairs * rows * rows,
        ),
        name="attend_back",
    )(joint, joint, joint, hot, bar, total, context, grad_context)


def row_mean(values):
    return jnp.mean(values, axis=-1, keepdims=True)


def normalize(rows_in):
    centered = rows_in - row_mean(rows_in)
    inverse = lax.rsqrt(row_mean(centered * centered) + epsilon)
    return centered * inverse, inverse


def normalize_back(grads, normal, inverse, gain):
    scaled = grads * gain
    return inverse * (scaled - row_mean(scaled) - normal * row_mean(scaled * normal))


def layer_forward(inputs, hot, bar, params, keep):
    w_qkv, w_out, w_up, w_down, gains, biases, up_bias = params
    width = inputs.shape[1]
    joint_bias = jnp.concatenate([biases[0], jnp.zeros_like(biases[0]), biases[1]])
    joint = (matmul(inputs, w_qkv) + joint_bias).astype(bf16)
    context, total = attend(joint, hot, bar)
    mixed = inputs.astype(f32) + (matmul(context, w_out) + biases[2])
    normal_one, inverse_one = normalize(mixed)
    hidden = (normal_one * gains[0] + biases[3]).astype(bf16)
    upper = matmul(hidden, w_up) + up_bias
    half = 0.5 * (1.0 + lax.erf(upper * 0.7071067811865476))
    activated = (upper * half).astype(bf16)
    slope = None
    if keep:
        bell = jnp.exp(upper * upper * -0.5) * 0.3989422804014327
        slope = (half + upper * bell).astype(bf16)
    summed = hidden.astype(f32) + (matmul(activated, w_down) + biases[4])
    normal_two, inverse_two = normalize(summed)
    result = (normal_two * gains[1] + biases[5]).astype(bf16)
    if not keep:
        return result
    stored = dict(
        inputs=inputs,
        joint=joint,
        context=context,
        total=total,
        normal_one=normal_one.astype(bf16),
        inverse_one=inverse_one,
        hidden=hidden,
        activated=activated,
        slope=slope,
        normal_two=normal_two.astype(bf16),
        inverse_two=inverse_two,
    )
    return result, stored


def layer_backward(grad_result, hot, bar, params, stored, keep):
    w_qkv, w_out, w_up, w_down, gains, biases, up_bias = params
    width = grad_result.shape[1]
    grad_result = grad_result.astype(f32)
    normal_two = stored["normal_two"].astype(f32)
    grad_summed = normalize_back(grad_result, normal_two, stored["inverse_two"], gains[1])
    grad_branch = grad_summed.astype(bf16)
    grad_activated = matmul_t(grad_branch, w_down)
    grad_upper = (grad_activated * stored["slope"].astype(f32)).astype(bf16)
    grad_hidden = grad_summed + matmul_t(grad_upper, w_up)
    normal_one = stored["normal_one"].astype(f32)
    grad_mixed = normalize_back(grad_hidden, normal_one, stored["inverse_one"], gains[0])
    grad_attn = grad_mixed.astype(bf16)
    grad_context = matmul_t(grad_attn, w_out).astype(bf16)
    grad_joint = attend_back(
        stored["joint"], hot, bar, stored["total"], stored["context"], grad_context
    )
    joined = jnp.concatenate([grad_joint[0], grad_joint[1], grad_joint[2]], axis=1)
    grad_inputs = (grad_mixed + matmul_t(joined, w_qkv)).astype(bf16)
    if not keep:
        return grad_inputs
    column = lambda values: jnp.sum(values.astype(f32), axis=0)
    joined_sums = column(joined)
    smalls = jnp.concatenate(
        [
            jnp.stack(
                [
                    column(grad_hidden * normal_one),
                    column(grad_result * normal_two),
                    joined_sums[:width],
                    joined_sums[2 * width :],
                    column(grad_attn),
                    column(grad_hidden),
                    column(grad_branch),
                    column(grad_result),
                ]
            ),
            column(grad_upper).reshape(-1, width),
        ]
    )
    used = dict(
        grad_branch=grad_branch, grad_upper=grad_upper, grad_attn=grad_attn, grad_joint=joined
    )
    return grad_inputs, used, smalls


def spread_features(values, shards, reps):
    lead = values.shape[:-1]
    rows = values.shape[-1] // (shards * reps * FF_BLOCKS)
    split = values.reshape(lead + (shards, reps, FF_BLOCKS, rows))
    at = len(lead)
    order = tuple(range(at)) + (at + 2, at, at + 1, at + 3)
    return split.transpose(order).reshape(values.shape)


def restore_features(values, shards, reps):
    lead = values.shape[:-1]
    rows = values.shape[-1] // (shards * reps * FF_BLOCKS)
    split = values.reshape(lead + (FF_BLOCKS, shards, reps, rows))
    at = len(lead)
    order = tuple(range(at)) + (at + 1, at + 2, at, at + 3)
    return split.transpose(order).reshape(values.shape)


def half_of(values, rep, reps, axis=0):
    size = values.shape[axis] // reps
    return lax.dynamic_slice_in_dim(values, rep * size, size, axis)


def gather_params(w_qkv, w_out, w_up, w_down, norm_gains, biases, up_bias):
    shards, reps = lax.axis_size("shard"), lax.axis_size("rep")
    rep = lax.axis_index("rep")
    width = w_out.shape[1]
    rows = w_out.shape[0] // reps
    ff = w_up.shape[1]
    part = norm_gains.shape[1]
    down = half_of(w_down, rep, reps).reshape(FF_BLOCKS, rows, width)
    down = down.transpose(1, 0, 2).reshape(rows, FF_BLOCKS * width)
    small = jnp.concatenate([norm_gains, biases, up_bias.reshape(-1, part)])
    kinds = small.shape[0]
    small = half_of(small, rep, reps).reshape(-1)
    small = jnp.pad(small, (0, rows * PAIR - small.shape[0])).reshape(rows, PAIR)
    packed = jnp.concatenate(
        [
            half_of(w_qkv, rep, reps),
            half_of(w_out, rep, reps),
            spread_features(half_of(w_up, rep, reps), shards, reps),
            down,
            small,
        ],
        axis=1,
    )
    whole = lax.all_gather(packed, ("shard", "rep"), axis=0, tiled=True)
    edges = [3 * width, 4 * width, 4 * width + ff, 4 * width + 2 * ff]
    small = whole[:, edges[3] :].reshape(shards * reps, rows * PAIR)
    small = small[:, : kinds // reps * part].reshape(shards, kinds, part).astype(f32)
    gains = small[:, :2].transpose(1, 0, 2).reshape(2, width)
    shifts = small[:, 2:8].transpose(1, 0, 2).reshape(6, width)
    up_shift = spread_features(small[:, 8:].reshape(ff), shards, reps)
    w_down_whole = whole[:, edges[2] : edges[3]].reshape(width, FF_BLOCKS, width)
    w_down_whole = w_down_whole.transpose(1, 0, 2).reshape(ff, width)
    return (
        whole[:, : edges[0]],
        whole[:, edges[0] : edges[1]],
        whole[:, edges[1] : edges[2]],
        w_down_whole,
        gains,
        shifts,
        up_shift,
    )


def ring_order(count):
    return list(range(0, count, 2)) + list(range(1, count, 2))[::-1]


def reduce_rows(terms):
    shards, reps = lax.axis_size("shard"), lax.axis_size("rep")
    rep, shard = lax.axis_index("rep"), lax.axis_index("shard")
    swap = [(i, (i + 1) % reps) for i in range(reps)]
    pick = lambda values, at, axis: lax.dynamic_index_in_dim(values, at, axis, keepdims=False)
    own = pick(terms, rep, 1)
    other = lax.ppermute(pick(terms, 1 - rep, 1), "rep", swap)
    if shards > LONGEST_RING:
        total = lax.psum_scatter(own + other, "shard", scatter_dimension=0, tiled=True)
        return total[0].astype(f32)
    order = ring_order(shards)
    places = [order.index(i) for i in range(shards)]
    place = jnp.asarray(places, jnp.int32)[shard]
    order_table = jnp.asarray(order, jnp.int32)
    way = 1 - 2 * rep
    route = []
    for i in range(shards):
        here, there = order[i], order[(i + 1) % shards]
        route.append((here * reps, there * reps))
        route.append((there * reps + 1, here * reps + 1))
    arrived = None
    for step in range(shards):
        target = order_table[(place - way * (1 + step)) % shards]
        total = pick(own, target, 0).astype(f32) + pick(other, target, 0).astype(f32)
        if arrived is not None:
            total = total + arrived.astype(f32)
        if step < shards - 1:
            arrived = lax.ppermute(total.astype(bf16), ("shard", "rep"), route)
    return total


def both_halves(half):
    reps, rep = lax.axis_size("rep"), lax.axis_index("rep")
    swap = [(i, (i + 1) % reps) for i in range(reps)]
    other = lax.ppermute(half.astype(bf16), "rep", swap).astype(f32)
    return jnp.where(rep == 0, jnp.stack([half, other]), jnp.stack([other, half]))


def on_device(
    boundary_in, segment_ids, keep_mask, w_qkv, w_out, w_up, w_down, norm_gains, biases, up_bias
):
    shards, reps = lax.axis_size("shard"), lax.axis_size("rep")
    is_first = lax.axis_index("section") == 0
    tokens = boundary_in[0]
    width = tokens.shape[1]
    row_count = tokens.shape[0] // MICRO
    rows = w_out.shape[1] // reps
    params = gather_params(
        w_qkv[0], w_out[0], w_up[0], w_down[0], norm_gains[0], biases[0], up_bias[0]
    )
    codes = segment_ids * 2 + keep_mask
    lane = lax.broadcasted_iota(jnp.int32, (row_count, PAIR), 1) % HEAD
    masks = []
    for micro in range(MICRO):
        same = codes[micro][:, None] == lane
        hot = same.astype(bf16)
        bar = jnp.where(same | (lane >= CODES), 0.0, masked_score).astype(bf16)
        masks.append((hot, bar))
    own = [tokens[micro * row_count : (micro + 1) * row_count] for micro in range(MICRO)]

    sent = []
    for micro in range(MICRO):
        middle = layer_forward(own[micro], *masks[micro], params, False)
        sent.append(lax.ppermute(middle, "section", [(0, 1)]))
    outputs, stash = [], []
    for micro in range(MICRO):
        inputs = jnp.where(is_first, own[micro], sent[micro])
        result, stored = layer_forward(inputs, *masks[micro], params, True)
        outputs.append(result)
        stash.append(stored)
    sent = []
    for micro in range(MICRO):
        grads = layer_backward(own[micro], *masks[micro], params, stash[micro], False)
        sent.append(lax.ppermute(grads, "section", [(1, 0)]))
    grads_back, used, smalls = [], [], None
    for micro in range(MICRO):
        grads = jnp.where(is_first, sent[micro], own[micro])
        grad_inputs, terms, sums = layer_backward(
            grads, *masks[micro], params, stash[micro], True
        )
        grads_back.append(grad_inputs)
        used.append(terms)
        smalls = sums if smalls is None else smalls + sums

    def weight_grad(left, right):
        lefts = jnp.concatenate([stored[left] for stored in stash])
        rights = jnp.concatenate([terms[right] for terms in used])
        return tmatmul(lefts, rights).astype(bf16)

    grad_down = weight_grad("activated", "grad_branch")
    grad_down = grad_down.reshape(FF_BLOCKS, shards, reps, rows, width).transpose(1, 2, 0, 3, 4)
    grad_up = weight_grad("hidden", "grad_upper").reshape(shards, reps, rows, -1)
    grad_out = weight_grad("context", "grad_attn").reshape(shards, reps, rows, width)
    grad_qkv = weight_grad("inputs", "grad_joint").reshape(shards, reps, rows, 3 * width)
    part = width // shards
    small = jnp.concatenate(
        [
            smalls[:8].reshape(8, shards, part).transpose(1, 0, 2),
            restore_features(smalls[8:].reshape(-1), shards, reps).reshape(shards, -1, part),
        ],
        axis=1,
    )
    kinds = small.shape[1]
    small = small.reshape(shards, reps, -1)
    used_part = small.shape[2]
    small = jnp.pad(small, ((0, 0), (0, 0), (0, rows * PAIR - used_part)))
    small = small.reshape(shards, reps, rows, PAIR).astype(bf16)

    down_total = both_halves(reduce_rows(grad_down))
    up_total = both_halves(restore_features(reduce_rows(grad_up), shards, reps))
    last_total = both_halves(
        reduce_rows(jnp.concatenate([grad_qkv, grad_out, small], axis=3))
    )
    small = last_total[:, :, 4 * width :].reshape(reps, -1)[:, :used_part]
    small = small.reshape(kinds, part)
    boundary_out = jnp.where(
        is_first, jnp.concatenate(grads_back, axis=0), jnp.concatenate(outputs, axis=0)
    )
    joined = lambda values: values.reshape((1, -1) + values.shape[2:])
    return (
        boundary_out[None],
        joined(last_total[:, :, : 3 * width]),
        joined(last_total[:, :, 3 * width : 4 * width]),
        joined(up_total),
        down_total.reshape(1, -1, width),
        small[:2][None],
        small[2:8][None],
        small[8:].reshape(1, -1),
    )


def solution(mesh):
    placed = (
        P("section", ("shard", "rep"), None),
        P(("shard", "rep"), None),
        P(("shard", "rep"), None),
        P("section", "shard", None),
        P("section", "shard", None),
        P("section", "shard", None),
        P("section", "shard", None),
        P("section", None, "shard"),
        P("section", None, "shard"),
        P("section", "shard"),
    )
    return jax.shard_map(
        on_device,
        mesh=mesh,
        in_specs=placed,
        out_specs=(
            P("section", ("shard", "rep"), None),
            P("section", "shard", None),
            P("section", "shard", None),
            P("section", "shard", None),
            P("section", "shard", None),
            P("section", None, "shard"),
            P("section", None, "shard"),
            P("section", "shard"),
        ),
        check_vma=False,
    )
```

```python
import functools

import jax
import jax.numpy as jnp
from jax import lax
from jax.experimental import pallas as pl
from jax.experimental.pallas import tpu as pltpu
from jax.sharding import PartitionSpec as P

HEAD = 64
MICRO = 2
PAIR = 2 * HEAD
CODES = 16
FF_BLOCKS = 4
LONGEST_RING = 16

epsilon = 1e-12
masked_score = -1e30
scale_head = HEAD ** (-0.5)


f32 = jnp.float32
bf16 = jnp.bfloat16


def matmul(left, right):
    return jnp.dot(left, right, preferred_element_type=f32)


def matmul_t(left, right):
    return lax.dot_general(left, right, (((1,), (1,)), ((), ())), preferred_element_type=f32)


def tmatmul(left, right):
    return lax.dot_general(left, right, (((0,), (0,)), ((), ())), preferred_element_type=f32)


def lanes_of(rows):
    return lax.broadcasted_iota(jnp.int32, (rows, PAIR), 1)


def attend_kernel(q_ref, k_ref, v_ref, hot_ref, bar_ref, context_ref, total_ref):
    rows = q_ref.shape[0]
    lane = lanes_of(rows)
    queries = q_ref[...] * scale_head
    keys_rows = k_ref[...]
    values_rows = v_ref[...]
    hot = hot_ref[...]
    bar = bar_ref[...]
    ones = jnp.ones_like(values_rows)
    contexts = []
    totals = []
    for head in range(2):
        own = (lane < HEAD) if head == 0 else (lane >= HEAD)
        scores = matmul_t(jnp.where(own, queries, hot), jnp.where(own, keys_rows, bar))
        top = jnp.max(scores, axis=1, keepdims=True)
        exponent = jnp.exp(scores - top).astype(bf16)
        both = matmul(exponent, jnp.where(own, values_rows, ones))
        row_total = pltpu.roll(both, HEAD, 1)
        contexts.append(both / row_total)
        totals.append(top + jnp.log(row_total))
    first = lane < HEAD
    context_ref[...] = jnp.where(first, contexts[0], contexts[1]).astype(bf16)
    total_ref[...] = jnp.where(first, totals[0], totals[1])


def attend(joint, hot, bar):
    rows, width = joint.shape[0], joint.shape[1] // 3
    pairs = width // PAIR
    block = lambda shift: pl.BlockSpec((rows, PAIR), lambda i: (0, shift + i))
    fixed = pl.BlockSpec((rows, PAIR), lambda i: (0, 0))
    return pl.pallas_call(
        attend_kernel,
        grid=(pairs,),
        in_specs=[block(0), block(pairs), block(2 * pairs), fixed, fixed],
        out_specs=[block(0), block(0)],
        out_shape=(
            jax.ShapeDtypeStruct((rows, width), bf16),
            jax.ShapeDtypeStruct((rows, width), f32),
        ),
        cost_estimate=pl.CostEstimate(
            flops=16 * rows * rows * width,
            bytes_accessed=12 * rows * width,
            transcendentals=2 * pairs * rows * rows,
        ),
        name="attend",
    )(joint, joint, joint, hot, bar)


def split_two(values):
    high = values.astype(bf16)
    return high, (values - high.astype(f32)).astype(bf16)


def attend_back_kernel(
    q_ref, k_ref, v_ref, hot_ref, bar_ref, total_ref, context_ref, grad_ref, out_ref, sums_ref
):
    rows = q_ref.shape[0]
    lane = lanes_of(rows)
    first = lane < HEAD
    queries = q_ref[...] * scale_head
    keys_rows = k_ref[...]
    values_rows = v_ref[...]
    grads = grad_ref[...]
    hot = hot_ref[...]
    bar = bar_ref[...]
    total_high, total_low = split_two(pltpu.roll(total_ref[...], HEAD, 1))
    product = grads.astype(f32) * context_ref[...].astype(f32)
    outs = []
    for head in range(2):
        own = first if head == 0 else jnp.logical_not(first)
        base = HEAD if head == 0 else 0
        high_lane = lane == base + CODES
        low_lane = lane == base + CODES + 1
        extra = jnp.where(high_lane, total_high, jnp.where(low_lane, total_low, hot))
        row_sum = jnp.sum(jnp.where(own, product, 0.0), axis=1, keepdims=True)
        sum_high, sum_low = split_two(jnp.broadcast_to(row_sum, product.shape))
        zeros = jnp.zeros_like(grads)
        grad_extra = jnp.where(high_lane, sum_high, jnp.where(low_lane, sum_low, zeros))
        minus = jnp.where(jnp.logical_or(high_lane, low_lane), -jnp.ones_like(grads), zeros)
        key_extra = jnp.where(jnp.logical_or(high_lane, low_lane), minus, bar)
        scores = matmul_t(jnp.where(own, keys_rows, key_extra), jnp.where(own, queries, extra))
        soft = jnp.exp(scores)
        grad_soft = matmul_t(
            jnp.where(own, values_rows, minus), jnp.where(own, grads, grad_extra)
        )
        grad_scores = (soft * grad_soft).astype(bf16)
        grad_values = matmul(soft.astype(bf16), grads)
        grad_keys = matmul(grad_scores, queries)
        grad_queries = tmatmul(grad_scores, keys_rows) * scale_head
        outs.append((grad_queries, grad_keys, grad_values))
    for place in range(3):
        both = jnp.where(first, outs[0][place], outs[1][place]).astype(bf16)
        out_ref[place] = both
        sums_ref[place] = jnp.sum(both.astype(f32), axis=0, keepdims=True)


def attend_back(joint, hot, bar, total, context, grad_context):
    rows, width = context.shape
    pairs = width // PAIR
    block = lambda shift: pl.BlockSpec((rows, PAIR), lambda i: (0, shift + i))
    fixed = pl.BlockSpec((rows, PAIR), lambda i: (0, 0))
    return pl.pallas_call(
        attend_back_kernel,
        grid=(pairs,),
        in_specs=[block(0), block(pairs), block(2 * pairs), fixed, fixed]
        + [block(0), block(0), block(0)],
        out_specs=[
            pl.BlockSpec((3, rows, PAIR), lambda i: (0, 0, i)),
            pl.BlockSpec((3, 1, PAIR), lambda i: (0, 0, i)),
        ],
        out_shape=(
            jax.ShapeDtypeStruct((3, rows, width), bf16),
            jax.ShapeDtypeStruct((3, 1, width), f32),
        ),
        cost_estimate=pl.CostEstimate(
            flops=40 * rows * rows * width,
            bytes_accessed=20 * rows * width,
            transcendentals=2 * pairs * rows * rows,
        ),
        name="attend_back",
    )(joint, joint, joint, hot, bar, total, context, grad_context)


FF_TILE = 512


def row_mean(values):
    return jnp.mean(values, axis=-1, keepdims=True)


def column_sum(values):
    return jnp.sum(values, axis=0, keepdims=True)


def erf_of(values):
    return lax.erf(values)


def normalize(rows_in):
    centered = rows_in - row_mean(rows_in)
    inverse = lax.rsqrt(row_mean(centered * centered) + epsilon)
    return centered * inverse, inverse


def normalize_back(grads, normal, inverse, gain):
    scaled = grads * gain
    return inverse * (scaled - row_mean(scaled) - normal * row_mean(scaled * normal))


def resident(*shape):
    return pl.BlockSpec(shape, lambda i: (0,) * len(shape))


def project_kernel(x_ref, w_ref, bias_ref, out_ref):
    out_ref[...] = (matmul(x_ref[...], w_ref[...]) + bias_ref[...]).astype(bf16)


def project(inputs, whole, bias):
    rows, width = inputs.shape
    tile = FF_TILE
    return pl.pallas_call(
        project_kernel,
        grid=(3 * width // tile,),
        in_specs=[
            resident(rows, width),
            pl.BlockSpec((width, tile), lambda i: (0, i)),
            pl.BlockSpec((1, tile), lambda i: (0, i)),
        ],
        out_specs=pl.BlockSpec((rows, tile), lambda i: (0, i)),
        out_shape=jax.ShapeDtypeStruct((rows, 3 * width), bf16),
        cost_estimate=pl.CostEstimate(
            flops=6 * rows * width * width,
            bytes_accessed=8 * rows * width + 6 * width * width,
            transcendentals=0,
        ),
        name="project",
    )(inputs, whole, bias)


def after_kernel(
    keep, x_ref, context_ref, out_w_ref, up_ref, down_ref, gain_ref, shift_ref, up_shift_ref, *refs
):
    if keep:
        result_ref, hidden_out, one_ref, inv_one_ref, act_ref, slope_ref, two_ref, inv_two_ref = refs[:8]
    else:
        result_ref = refs[0]
    hidden_ref, total_ref = refs[-2:]
    step = pl.program_id(0)

    @pl.when(step == 0)
    def _():
        mixed = x_ref[...].astype(f32) + matmul(context_ref[...], out_w_ref[...]) + shift_ref[2:3]
        normal, inverse = normalize(mixed)
        hidden = (normal * gain_ref[0:1] + shift_ref[3:4]).astype(bf16)
        hidden_ref[...] = hidden
        total_ref[...] = hidden.astype(f32) + shift_ref[4:5]
        if keep:
            hidden_out[...] = hidden
            one_ref[...] = normal.astype(bf16)
            inv_one_ref[...] = jnp.broadcast_to(inverse, inv_one_ref.shape)

    upper = matmul(hidden_ref[...], up_ref[...]) + up_shift_ref[...]
    half = 0.5 * (1.0 + erf_of(upper * 0.7071067811865476))
    activated = (upper * half).astype(bf16)
    if keep:
        act_ref[...] = activated
        bell = jnp.exp(upper * upper * -0.5) * 0.3989422804014327
        slope_ref[...] = (half + upper * bell).astype(bf16)
    total_ref[...] += matmul(activated, down_ref[...])

    @pl.when(step == pl.num_programs(0) - 1)
    def _():
        normal, inverse = normalize(total_ref[...])
        result_ref[...] = (normal * gain_ref[1:2] + shift_ref[5:6]).astype(bf16)
        if keep:
            two_ref[...] = normal.astype(bf16)
            inv_two_ref[...] = jnp.broadcast_to(inverse, inv_two_ref.shape)


def weight_specs(width, ff):
    tile = FF_TILE
    each = width // tile
    start = 4 * width // tile
    return [
        pl.BlockSpec((width, width), lambda i: (0, 3)),
        pl.BlockSpec((width, tile), lambda i: (0, start + i)),
        pl.BlockSpec((tile, width), lambda i: (i % each, 4 + ff // width + i // each)),
    ]


def after_attention(inputs, context, whole, gains, shifts, up_shift, keep):
    rows, width = inputs.shape
    ff = up_shift.shape[1]
    tile = FF_TILE
    full = resident(rows, width)
    stat = resident(rows, PAIR)
    wide = pl.BlockSpec((rows, tile), lambda i: (0, i))
    full_type = jax.ShapeDtypeStruct((rows, width), bf16)
    stat_type = jax.ShapeDtypeStruct((rows, PAIR), f32)
    wide_type = jax.ShapeDtypeStruct((rows, ff), bf16)
    specs, types = [full], [full_type]
    if keep:
        specs += [full, full, stat, wide, wide, full, stat]
        types += [full_type, full_type, stat_type, wide_type, wide_type, full_type, stat_type]
    return pl.pallas_call(
        functools.partial(after_kernel, keep),
        grid=(ff // tile,),
        in_specs=[full, full]
        + weight_specs(width, ff)
        + [resident(2, width), resident(6, width), pl.BlockSpec((1, tile), lambda i: (0, i))],
        out_specs=specs,
        out_shape=types,
        scratch_shapes=[pltpu.VMEM((rows, width), bf16), pltpu.VMEM((rows, width), f32)],
        cost_estimate=pl.CostEstimate(
            flops=2 * rows * width * (width + 2 * ff),
            bytes_accessed=2 * width * (width + 2 * ff) + 4 * rows * ff,
            transcendentals=rows * ff,
        ),
        name="after_attention",
    )(inputs, context, whole, whole, whole, gains, shifts, up_shift)


def before_kernel(
    keep, grad_ref, two_ref, inv_two_ref, slope_ref, one_ref, inv_one_ref,
    out_w_ref, up_ref, down_ref, gain_ref, *refs
):
    mixed_ref, context_ref = refs[:2]
    if keep:
        attn_ref, branch_out, upper_ref, sums_ref, upper_sum_ref = refs[2:7]
    branch_ref, total_ref = refs[-2:]
    step = pl.program_id(0)

    @pl.when(step == 0)
    def _():
        grads = grad_ref[...].astype(f32)
        normal = two_ref[...].astype(f32)
        grad_summed = normalize_back(grads, normal, inv_two_ref[:, 0:1], gain_ref[1:2])
        branch = grad_summed.astype(bf16)
        branch_ref[...] = branch
        total_ref[...] = grad_summed
        if keep:
            branch_out[...] = branch
            sums_ref[1:2] = column_sum(grads * normal)
            sums_ref[4:5] = column_sum(branch.astype(f32))
            sums_ref[5:6] = column_sum(grads)

    grad_upper = matmul_t(branch_ref[...], down_ref[...]) * slope_ref[...].astype(f32)
    grad_upper = grad_upper.astype(bf16)
    if keep:
        upper_ref[...] = grad_upper
        upper_sum_ref[...] = column_sum(grad_upper.astype(f32))
    total_ref[...] += matmul_t(grad_upper, up_ref[...])

    @pl.when(step == pl.num_programs(0) - 1)
    def _():
        grads = total_ref[...]
        normal = one_ref[...].astype(f32)
        grad_mixed = normalize_back(grads, normal, inv_one_ref[:, 0:1], gain_ref[0:1])
        attn = grad_mixed.astype(bf16)
        mixed_ref[...] = grad_mixed
        context_ref[...] = matmul_t(attn, out_w_ref[...]).astype(bf16)
        if keep:
            attn_ref[...] = attn
            sums_ref[0:1] = column_sum(grads * normal)
            sums_ref[2:3] = column_sum(attn.astype(f32))
            sums_ref[3:4] = column_sum(grads)


def before_attention(grads, stored, whole, gains, keep):
    rows, width = grads.shape
    ff = stored["slope"].shape[1]
    tile = FF_TILE
    full = resident(rows, width)
    stat = resident(rows, PAIR)
    wide = pl.BlockSpec((rows, tile), lambda i: (0, i))
    full_type = jax.ShapeDtypeStruct((rows, width), bf16)
    specs = [full, full]
    types = [jax.ShapeDtypeStruct((rows, width), f32), full_type]
    if keep:
        specs += [full, full, wide, resident(8, width), pl.BlockSpec((1, tile), lambda i: (0, i))]
        types += [
            full_type,
            full_type,
            jax.ShapeDtypeStruct((rows, ff), bf16),
            jax.ShapeDtypeStruct((8, width), f32),
            jax.ShapeDtypeStruct((1, ff), f32),
        ]
    return pl.pallas_call(
        functools.partial(before_kernel, keep),
        grid=(ff // tile,),
        in_specs=[full, full, stat, wide, full, stat]
        + weight_specs(width, ff)
        + [resident(2, width)],
        out_specs=specs,
        out_shape=types,
        scratch_shapes=[pltpu.VMEM((rows, width), bf16), pltpu.VMEM((rows, width), f32)],
        cost_estimate=pl.CostEstimate(
            flops=2 * rows * width * (width + 2 * ff),
            bytes_accessed=2 * width * (width + 2 * ff) + 4 * rows * ff,
            transcendentals=0,
        ),
        name="before_attention",
    )(
        grads, stored["normal_two"], stored["inverse_two"], stored["slope"],
        stored["normal_one"], stored["inverse_one"], whole, whole, whole, gains,
    )


def project_back_kernel(mixed_ref, joint_ref, w_ref, out_ref):
    width = joint_ref.shape[2]
    total = mixed_ref[...]
    for place in range(3):
        total = total + matmul_t(joint_ref[place], w_ref[:, place * width : (place + 1) * width])
    out_ref[...] = total.astype(bf16)


def project_back(grad_mixed, grad_joint, whole):
    rows, width = grad_mixed.shape
    tile = 256
    return pl.pallas_call(
        project_back_kernel,
        grid=(width // tile,),
        in_specs=[
            pl.BlockSpec((rows, tile), lambda i: (0, i)),
            resident(3, rows, width),
            pl.BlockSpec((tile, 3 * width), lambda i: (i, 0)),
        ],
        out_specs=pl.BlockSpec((rows, tile), lambda i: (0, i)),
        out_shape=jax.ShapeDtypeStruct((rows, width), bf16),
        cost_estimate=pl.CostEstimate(
            flops=6 * rows * width * width,
            bytes_accessed=12 * rows * width + 6 * width * width,
            transcendentals=0,
        ),
        name="project_back",
    )(grad_mixed, grad_joint, whole)


def weight_grad_kernel(left_one, left_two, right_one, right_two, out_ref):
    total = tmatmul(left_one[...], right_one[...]) + tmatmul(left_two[...], right_two[...])
    out_ref[...] = total.astype(bf16)


def weight_grad(lefts, rights, tile_rows=512, tile_columns=1024):
    rows, height = lefts[0].shape
    stacked = rights[0].ndim == 3
    columns = rights[0].shape[-1]
    parts = rights[0].shape[0] if stacked else columns // tile_columns
    across = parts * columns // tile_columns if stacked else parts
    left = pl.BlockSpec((rows, tile_rows), lambda j, i: (0, i))
    if stacked:
        right = pl.BlockSpec((None, rows, tile_columns), lambda j, i: (j, 0, 0))
    else:
        right = pl.BlockSpec((rows, tile_columns), lambda j, i: (0, j))
    return pl.pallas_call(
        weight_grad_kernel,
        grid=(across, height // tile_rows),
        in_specs=[left, left, right, right],
        out_specs=pl.BlockSpec((tile_rows, tile_columns), lambda j, i: (i, j)),
        out_shape=jax.ShapeDtypeStruct((height, across * tile_columns), bf16),
        cost_estimate=pl.CostEstimate(
            flops=4 * rows * height * across * tile_columns,
            bytes_accessed=4 * rows * (height + across * tile_columns)
            + 2 * height * across * tile_columns,
            transcendentals=0,
        ),
        name="weight_grad",
    )(*lefts, *rights)


def layer_forward(inputs, hot, bar, params, keep):
    whole, gains, shifts, up_shift = params
    bias = jnp.concatenate([shifts[0], jnp.zeros_like(shifts[0]), shifts[1]])[None]
    joint = project(inputs, whole, bias)
    context, total = attend(joint, hot, bar)
    made = after_attention(inputs, context, whole, gains, shifts, up_shift, keep)
    if not keep:
        return made[0]
    names = (
        "hidden", "normal_one", "inverse_one", "activated", "slope", "normal_two", "inverse_two"
    )
    stored = dict(zip(names, made[1:]))
    stored.update(inputs=inputs, joint=joint, context=context, total=total)
    return made[0], stored


def layer_backward(grads, hot, bar, params, stored):
    whole, gains, shifts, up_shift = params
    made = before_attention(grads, stored, whole, gains, False)
    grad_joint, _ = attend_back(
        stored["joint"], hot, bar, stored["total"], stored["context"], made[1]
    )
    return project_back(made[0], grad_joint, whole)


def spread_features(values, shards, reps):
    lead = values.shape[:-1]
    rows = values.shape[-1] // (shards * reps * FF_BLOCKS)
    split = values.reshape(lead + (shards, reps, FF_BLOCKS, rows))
    at = len(lead)
    order = tuple(range(at)) + (at + 2, at, at + 1, at + 3)
    return split.transpose(order).reshape(values.shape)


def restore_features(values, shards, reps):
    lead = values.shape[:-1]
    rows = values.shape[-1] // (shards * reps * FF_BLOCKS)
    split = values.reshape(lead + (FF_BLOCKS, shards, reps, rows))
    at = len(lead)
    order = tuple(range(at)) + (at + 1, at + 2, at, at + 3)
    return split.transpose(order).reshape(values.shape)


def half_of(values, rep, reps, axis=0):
    size = values.shape[axis] // reps
    return lax.dynamic_slice_in_dim(values, rep * size, size, axis)


def gather_params(w_qkv, w_out, w_up, w_down, norm_gains, biases, up_bias):
    shards, reps = lax.axis_size("shard"), lax.axis_size("rep")
    rep = lax.axis_index("rep")
    width = w_out.shape[1]
    rows = w_out.shape[0] // reps
    ff = w_up.shape[1]
    part = norm_gains.shape[1]
    down = half_of(w_down, rep, reps).reshape(FF_BLOCKS, rows, width)
    down = down.transpose(1, 0, 2).reshape(rows, FF_BLOCKS * width)
    small = jnp.concatenate([norm_gains, biases, up_bias.reshape(-1, part)])
    kinds = small.shape[0]
    small = half_of(small, rep, reps).reshape(-1)
    small = jnp.pad(small, (0, rows * PAIR - small.shape[0])).reshape(rows, PAIR)
    packed = jnp.concatenate(
        [
            half_of(w_qkv, rep, reps),
            half_of(w_out, rep, reps),
            spread_features(half_of(w_up, rep, reps), shards, reps),
            down,
            small,
        ],
        axis=1,
    )
    whole = lax.all_gather(packed, ("shard", "rep"), axis=0, tiled=True)
    edges = [3 * width, 4 * width, 4 * width + ff, 4 * width + 2 * ff]
    small = whole[:, edges[3] :].reshape(shards * reps, rows * PAIR)
    small = small[:, : kinds // reps * part].reshape(shards, kinds, part).astype(f32)
    gains = small[:, :2].transpose(1, 0, 2).reshape(2, width)
    shifts = small[:, 2:8].transpose(1, 0, 2).reshape(6, width)
    up_shift = spread_features(small[:, 8:].reshape(ff), shards, reps)
    return whole, gains, shifts, up_shift[None]


def ring_order(count):
    return list(range(0, count, 2)) + list(range(1, count, 2))[::-1]


def reduce_rows(terms, at=0):
    shards, reps = lax.axis_size("shard"), lax.axis_size("rep")
    rep, shard = lax.axis_index("rep"), lax.axis_index("shard")
    swap = [(i, (i + 1) % reps) for i in range(reps)]
    pick = lambda values, at, axis: lax.dynamic_index_in_dim(values, at, axis, keepdims=False)
    own = pick(terms, rep, at + 1)
    other = lax.ppermute(pick(terms, 1 - rep, at + 1), "rep", swap)
    if shards > LONGEST_RING:
        return lax.psum_scatter(own + other, "shard", scatter_dimension=at).astype(f32)
    order = ring_order(shards)
    places = [order.index(i) for i in range(shards)]
    place = jnp.asarray(places, jnp.int32)[shard]
    order_table = jnp.asarray(order, jnp.int32)
    way = 1 - 2 * rep
    route = []
    for i in range(shards):
        here, there = order[i], order[(i + 1) % shards]
        route.append((here * reps, there * reps))
        route.append((there * reps + 1, here * reps + 1))
    arrived = None
    for step in range(shards):
        target = order_table[(place - way * (1 + step)) % shards]
        total = pick(own, target, at).astype(f32) + pick(other, target, at).astype(f32)
        if arrived is not None:
            total = total + arrived.astype(f32)
        if step < shards - 1:
            arrived = lax.ppermute(total.astype(bf16), ("shard", "rep"), route)
    return total


def both_halves(half):
    reps, rep = lax.axis_size("rep"), lax.axis_index("rep")
    swap = [(i, (i + 1) % reps) for i in range(reps)]
    other = lax.ppermute(half.astype(bf16), "rep", swap).astype(f32)
    return jnp.where(rep == 0, jnp.stack([half, other]), jnp.stack([other, half]))


def on_device(
    boundary_in, segment_ids, keep_mask, w_qkv, w_out, w_up, w_down, norm_gains, biases, up_bias
):
    shards, reps = lax.axis_size("shard"), lax.axis_size("rep")
    is_first = lax.axis_index("section") == 0
    tokens = boundary_in[0]
    width = tokens.shape[1]
    row_count = tokens.shape[0] // MICRO
    rows = w_out.shape[1] // reps
    params = gather_params(
        w_qkv[0], w_out[0], w_up[0], w_down[0], norm_gains[0], biases[0], up_bias[0]
    )
    codes = segment_ids * 2 + keep_mask
    lane = lax.broadcasted_iota(jnp.int32, (row_count, PAIR), 1) % HEAD
    masks = []
    for micro in range(MICRO):
        same = codes[micro][:, None] == lane
        hot = same.astype(bf16)
        bar = jnp.where(same | (lane >= CODES), 0.0, masked_score).astype(bf16)
        masks.append((hot, bar))
    own = [tokens[micro * row_count : (micro + 1) * row_count] for micro in range(MICRO)]

    after = lax.optimization_barrier
    whole, gains = params[:2]

    sent, entries = [], list(own)
    for micro in range(MICRO):
        middle = layer_forward(entries[micro], *masks[micro], params, False)
        place = (micro + 1) % MICRO
        middle, entries[place] = after((middle, entries[place]))
        sent.append(lax.ppermute(middle, "section", [(0, 1)]))
    outputs, stash, sent_back = [], [], []
    starts = [entries[0], own[1]]
    for micro in range(MICRO):
        inputs = jnp.where(is_first, starts[micro], sent[micro])
        result, stored = layer_forward(inputs, *masks[micro], params, True)
        result, grads = after((result, own[micro]))
        outputs.append(result)
        stash.append(stored)
        grads = layer_backward(grads, *masks[micro], params, stored)
        if micro + 1 < MICRO:
            grads, starts[micro + 1] = after((grads, starts[micro + 1]))
        else:
            grads, entries[0] = after((grads, own[0]))
        sent_back.append(lax.ppermute(grads, "section", [(1, 0)]))

    def grad_of(left, right):
        return weight_grad([stored[left] for stored in stash], [terms[right] for terms in used])

    made = []
    for micro in range(MICRO):
        grads = jnp.where(is_first, sent_back[micro], entries[0] if micro == 0 else own[micro])
        made.append(before_attention(grads, stash[micro], whole, gains, True))
    used = [dict(grad_attn=m[2], grad_branch=m[3], grad_upper=m[4]) for m in made]
    grad_down = grad_of("activated", "grad_branch")
    grad_down = grad_down.reshape(FF_BLOCKS, shards, reps, rows, width)
    grad_up = grad_of("hidden", "grad_upper").reshape(shards, reps, rows, -1)
    grad_out = grad_of("context", "grad_attn").reshape(shards, reps, rows, width)
    smalls = []
    for micro in range(MICRO):
        stored = stash[micro]
        grad_joint, sums = attend_back(
            stored["joint"], *masks[micro], stored["total"], stored["context"], made[micro][1]
        )
        used[micro]["grad_joint"] = grad_joint
        base = made[micro][5]
        smalls.append(
            jnp.concatenate(
                [base[:2], sums[0], sums[2], base[2:6], made[micro][6].reshape(-1, width)]
            )
        )
    smalls = sum(smalls[1:], smalls[0])
    grad_qkv = grad_of("inputs", "grad_joint").reshape(shards, reps, rows, 3 * width)
    grads_back = [
        project_back(made[micro][0], used[micro]["grad_joint"], whole) for micro in range(MICRO)
    ]
    part = width // shards
    small = jnp.concatenate(
        [
            smalls[:8].reshape(8, shards, part).transpose(1, 0, 2),
            restore_features(smalls[8:].reshape(-1), shards, reps).reshape(shards, -1, part),
        ],
        axis=1,
    )
    kinds = small.shape[1]
    small = small.reshape(shards, reps, -1)
    used_part = small.shape[2]
    small = jnp.pad(small, ((0, 0), (0, 0), (0, rows * PAIR - used_part)))
    small = small.reshape(shards, reps, rows, PAIR).astype(bf16)

    down_total = both_halves(reduce_rows(grad_down, 1))
    up_total = both_halves(restore_features(reduce_rows(grad_up), shards, reps))
    last_total = both_halves(
        reduce_rows(jnp.concatenate([grad_qkv, grad_out, small], axis=3))
    )
    small = last_total[:, :, 4 * width :].reshape(reps, -1)[:, :used_part]
    small = small.reshape(kinds, part)
    boundary_out = jnp.where(
        is_first, jnp.concatenate(grads_back, axis=0), jnp.concatenate(outputs, axis=0)
    )
    joined = lambda values: values.reshape((1, -1) + values.shape[2:])
    return (
        boundary_out[None],
        joined(last_total[:, :, : 3 * width]),
        joined(last_total[:, :, 3 * width : 4 * width]),
        joined(up_total),
        down_total.reshape(1, -1, width),
        small[:2][None],
        small[2:8][None],
        small[8:].reshape(1, -1),
    )


def solution(mesh):
    placed = (
        P("section", ("shard", "rep"), None),
        P(("shard", "rep"), None),
        P(("shard", "rep"), None),
        P("section", "shard", None),
        P("section", "shard", None),
        P("section", "shard", None),
        P("section", "shard", None),
        P("section", None, "shard"),
        P("section", None, "shard"),
        P("section", "shard"),
    )
    return jax.shard_map(
        on_device,
        mesh=mesh,
        in_specs=placed,
        out_specs=(
            P("section", ("shard", "rep"), None),
            P("section", "shard", None),
            P("section", "shard", None),
            P("section", "shard", None),
            P("section", "shard", None),
            P("section", None, "shard"),
            P("section", None, "shard"),
            P("section", "shard"),
        ),
        check_vma=False,
    )
```

```python
import functools

import jax
import jax.numpy as jnp
from jax import lax
from jax.experimental import pallas as pl
from jax.experimental.pallas import tpu as pltpu
from jax.sharding import PartitionSpec as P

HEAD = 64
MICRO = 2
PAIR = 2 * HEAD
CODES = 16
FF_BLOCKS = 4
LONGEST_RING = 16

epsilon = 1e-12
masked_score = -1e30
scale_head = HEAD ** (-0.5)


f32 = jnp.float32
bf16 = jnp.bfloat16


def matmul(left, right):
    return jnp.dot(left, right, preferred_element_type=f32)


def matmul_t(left, right):
    return lax.dot_general(left, right, (((1,), (1,)), ((), ())), preferred_element_type=f32)


def tmatmul(left, right):
    return lax.dot_general(left, right, (((0,), (0,)), ((), ())), preferred_element_type=f32)


def lanes_of(rows):
    return lax.broadcasted_iota(jnp.int32, (rows, PAIR), 1)


def attend_kernel(q_ref, k_ref, v_ref, hot_ref, bar_ref, context_ref, total_ref):
    rows = q_ref.shape[0]
    lane = lanes_of(rows)
    queries = q_ref[...] * scale_head
    keys_rows = k_ref[...]
    values_rows = v_ref[...]
    hot = hot_ref[...]
    bar = bar_ref[...]
    ones = jnp.ones_like(values_rows)
    contexts = []
    totals = []
    for head in range(2):
        own = (lane < HEAD) if head == 0 else (lane >= HEAD)
        scores = matmul_t(jnp.where(own, queries, hot), jnp.where(own, keys_rows, bar))
        top = jnp.max(scores, axis=1, keepdims=True)
        exponent = jnp.exp(scores - top).astype(bf16)
        both = matmul(exponent, jnp.where(own, values_rows, ones))
        row_total = pltpu.roll(both, HEAD, 1)
        contexts.append(both / row_total)
        totals.append(top + jnp.log(row_total))
    first = lane < HEAD
    context_ref[...] = jnp.where(first, contexts[0], contexts[1]).astype(bf16)
    total_ref[...] = jnp.where(first, totals[0], totals[1])


def attend(joint, hot, bar):
    rows, width = joint.shape[0], joint.shape[1] // 3
    pairs = width // PAIR
    block = lambda shift: pl.BlockSpec((rows, PAIR), lambda i: (0, shift + i))
    fixed = pl.BlockSpec((rows, PAIR), lambda i: (0, 0))
    return pl.pallas_call(
        attend_kernel,
        grid=(pairs,),
        in_specs=[block(0), block(pairs), block(2 * pairs), fixed, fixed],
        out_specs=[block(0), block(0)],
        out_shape=(
            jax.ShapeDtypeStruct((rows, width), bf16),
            jax.ShapeDtypeStruct((rows, width), f32),
        ),
        cost_estimate=pl.CostEstimate(
            flops=16 * rows * rows * width,
            bytes_accessed=12 * rows * width,
            transcendentals=2 * pairs * rows * rows,
        ),
        name="attend",
    )(joint, joint, joint, hot, bar)


def split_two(values):
    high = values.astype(bf16)
    return high, (values - high.astype(f32)).astype(bf16)


def attend_back_kernel(
    q_ref, k_ref, v_ref, hot_ref, bar_ref, total_ref, context_ref, grad_ref, out_ref, sums_ref
):
    rows = q_ref.shape[0]
    lane = lanes_of(rows)
    first = lane < HEAD
    queries = q_ref[...] * scale_head
    keys_rows = k_ref[...]
    values_rows = v_ref[...]
    grads = grad_ref[...]
    hot = hot_ref[...]
    bar = bar_ref[...]
    total_high, total_low = split_two(pltpu.roll(total_ref[...], HEAD, 1))
    product = grads.astype(f32) * context_ref[...].astype(f32)
    outs = []
    for head in range(2):
        own = first if head == 0 else jnp.logical_not(first)
        base = HEAD if head == 0 else 0
        high_lane = lane == base + CODES
        low_lane = lane == base + CODES + 1
        extra = jnp.where(high_lane, total_high, jnp.where(low_lane, total_low, hot))
        row_sum = jnp.sum(jnp.where(own, product, 0.0), axis=1, keepdims=True)
        sum_high, sum_low = split_two(jnp.broadcast_to(row_sum, product.shape))
        zeros = jnp.zeros_like(grads)
        grad_extra = jnp.where(high_lane, sum_high, jnp.where(low_lane, sum_low, zeros))
        minus = jnp.where(jnp.logical_or(high_lane, low_lane), -jnp.ones_like(grads), zeros)
        key_extra = jnp.where(jnp.logical_or(high_lane, low_lane), minus, bar)
        scores = matmul_t(jnp.where(own, keys_rows, key_extra), jnp.where(own, queries, extra))
        soft = jnp.exp(scores)
        grad_soft = matmul_t(
            jnp.where(own, values_rows, minus), jnp.where(own, grads, grad_extra)
        )
        grad_scores = (soft * grad_soft).astype(bf16)
        grad_values = matmul(soft.astype(bf16), grads)
        grad_keys = matmul(grad_scores, queries)
        grad_queries = tmatmul(grad_scores, keys_rows) * scale_head
        outs.append((grad_queries, grad_keys, grad_values))
    for place in range(3):
        both = jnp.where(first, outs[0][place], outs[1][place]).astype(bf16)
        out_ref[place] = both
        sums_ref[place] = jnp.sum(both.astype(f32), axis=0, keepdims=True)


def attend_back(joint, hot, bar, total, context, grad_context):
    rows, width = context.shape
    pairs = width // PAIR
    block = lambda shift: pl.BlockSpec((rows, PAIR), lambda i: (0, shift + i))
    fixed = pl.BlockSpec((rows, PAIR), lambda i: (0, 0))
    return pl.pallas_call(
        attend_back_kernel,
        grid=(pairs,),
        in_specs=[block(0), block(pairs), block(2 * pairs), fixed, fixed]
        + [block(0), block(0), block(0)],
        out_specs=[
            pl.BlockSpec((3, rows, PAIR), lambda i: (0, 0, i)),
            pl.BlockSpec((3, 1, PAIR), lambda i: (0, 0, i)),
        ],
        out_shape=(
            jax.ShapeDtypeStruct((3, rows, width), bf16),
            jax.ShapeDtypeStruct((3, 1, width), f32),
        ),
        cost_estimate=pl.CostEstimate(
            flops=40 * rows * rows * width,
            bytes_accessed=20 * rows * width,
            transcendentals=2 * pairs * rows * rows,
        ),
        name="attend_back",
    )(joint, joint, joint, hot, bar, total, context, grad_context)


FF_TILE = 512


def row_mean(values):
    return jnp.mean(values, axis=-1, keepdims=True)


def column_sum(values):
    return jnp.sum(values, axis=0, keepdims=True)


def erf_of(values):
    return lax.erf(values)


def normalize(rows_in):
    centered = rows_in - row_mean(rows_in)
    inverse = lax.rsqrt(row_mean(centered * centered) + epsilon)
    return centered * inverse, inverse


def normalize_back(grads, normal, inverse, gain):
    scaled = grads * gain
    return inverse * (scaled - row_mean(scaled) - normal * row_mean(scaled * normal))


def resident(*shape):
    return pl.BlockSpec(shape, lambda i: (0,) * len(shape))


def project_kernel(x_ref, w_ref, bias_ref, out_ref):
    out_ref[...] = (matmul(x_ref[...], w_ref[...]) + bias_ref[...]).astype(bf16)


def project(inputs, whole, bias):
    rows, width = inputs.shape
    tile = FF_TILE
    return pl.pallas_call(
        project_kernel,
        grid=(3 * width // tile,),
        in_specs=[
            resident(rows, width),
            pl.BlockSpec((width, tile), lambda i: (0, i)),
            pl.BlockSpec((1, tile), lambda i: (0, i)),
        ],
        out_specs=pl.BlockSpec((rows, tile), lambda i: (0, i)),
        out_shape=jax.ShapeDtypeStruct((rows, 3 * width), bf16),
        cost_estimate=pl.CostEstimate(
            flops=6 * rows * width * width,
            bytes_accessed=8 * rows * width + 6 * width * width,
            transcendentals=0,
        ),
        name="project",
    )(inputs, whole, bias)


def after_kernel(
    keep, x_ref, context_ref, out_w_ref, up_ref, down_ref, gain_ref, shift_ref, up_shift_ref, *refs
):
    if keep:
        result_ref, hidden_out, one_ref, inv_one_ref, act_ref, slope_ref, two_ref, inv_two_ref = refs[:8]
    else:
        result_ref = refs[0]
    hidden_ref, total_ref = refs[-2:]
    step = pl.program_id(0)

    @pl.when(step == 0)
    def _():
        mixed = x_ref[...].astype(f32) + matmul(context_ref[...], out_w_ref[...]) + shift_ref[2:3]
        normal, inverse = normalize(mixed)
        hidden = (normal * gain_ref[0:1] + shift_ref[3:4]).astype(bf16)
        hidden_ref[...] = hidden
        total_ref[...] = hidden.astype(f32) + shift_ref[4:5]
        if keep:
            hidden_out[...] = hidden
            one_ref[...] = normal.astype(bf16)
            inv_one_ref[...] = jnp.broadcast_to(inverse, inv_one_ref.shape)

    upper = matmul(hidden_ref[...], up_ref[...]) + up_shift_ref[...]
    half = 0.5 * (1.0 + erf_of(upper * 0.7071067811865476))
    activated = (upper * half).astype(bf16)
    if keep:
        act_ref[...] = activated
        bell = jnp.exp(upper * upper * -0.5) * 0.3989422804014327
        slope_ref[...] = (half + upper * bell).astype(bf16)
    total_ref[...] += matmul(activated, down_ref[...])

    @pl.when(step == pl.num_programs(0) - 1)
    def _():
        normal, inverse = normalize(total_ref[...])
        result_ref[...] = (normal * gain_ref[1:2] + shift_ref[5:6]).astype(bf16)
        if keep:
            two_ref[...] = normal.astype(bf16)
            inv_two_ref[...] = jnp.broadcast_to(inverse, inv_two_ref.shape)


def weight_specs(width, ff):
    tile = FF_TILE
    each = width // tile
    return [
        pl.BlockSpec((width, width), lambda i: (0, 3)),
        pl.BlockSpec((width, tile), lambda i: (0, i)),
        pl.BlockSpec((tile, width), lambda i: (i % each, ff // width + i // each)),
    ]


def after_attention(inputs, context, params, keep):
    attn, mlp, gains, shifts, up_shift = params
    rows, width = inputs.shape
    ff = up_shift.shape[1]
    tile = FF_TILE
    full = resident(rows, width)
    stat = resident(rows, PAIR)
    wide = pl.BlockSpec((rows, tile), lambda i: (0, i))
    full_type = jax.ShapeDtypeStruct((rows, width), bf16)
    stat_type = jax.ShapeDtypeStruct((rows, PAIR), f32)
    wide_type = jax.ShapeDtypeStruct((rows, ff), bf16)
    specs, types = [full], [full_type]
    if keep:
        specs += [full, full, stat, wide, wide, full, stat]
        types += [full_type, full_type, stat_type, wide_type, wide_type, full_type, stat_type]
    return pl.pallas_call(
        functools.partial(after_kernel, keep),
        grid=(ff // tile,),
        in_specs=[full, full]
        + weight_specs(width, ff)
        + [resident(2, width), resident(6, width), pl.BlockSpec((1, tile), lambda i: (0, i))],
        out_specs=specs,
        out_shape=types,
        scratch_shapes=[pltpu.VMEM((rows, width), bf16), pltpu.VMEM((rows, width), f32)],
        cost_estimate=pl.CostEstimate(
            flops=2 * rows * width * (width + 2 * ff),
            bytes_accessed=2 * width * (width + 2 * ff) + 4 * rows * ff,
            transcendentals=rows * ff,
        ),
        name="after_attention",
    )(inputs, context, attn, mlp, mlp, gains, shifts, up_shift)


def before_kernel(
    keep, grad_ref, two_ref, inv_two_ref, slope_ref, one_ref, inv_one_ref,
    out_w_ref, up_ref, down_ref, gain_ref, *refs
):
    mixed_ref, context_ref = refs[:2]
    if keep:
        attn_ref, branch_out, upper_ref, sums_ref, upper_sum_ref = refs[2:7]
    branch_ref, total_ref = refs[-2:]
    step = pl.program_id(0)

    @pl.when(step == 0)
    def _():
        grads = grad_ref[...].astype(f32)
        normal = two_ref[...].astype(f32)
        grad_summed = normalize_back(grads, normal, inv_two_ref[:, 0:1], gain_ref[1:2])
        branch = grad_summed.astype(bf16)
        branch_ref[...] = branch
        total_ref[...] = grad_summed
        if keep:
            branch_out[...] = branch
            sums_ref[1:2] = column_sum(grads * normal)
            sums_ref[4:5] = column_sum(branch.astype(f32))
            sums_ref[5:6] = column_sum(grads)

    grad_upper = matmul_t(branch_ref[...], down_ref[...]) * slope_ref[...].astype(f32)
    grad_upper = grad_upper.astype(bf16)
    if keep:
        upper_ref[...] = grad_upper
        upper_sum_ref[...] = column_sum(grad_upper.astype(f32))
    total_ref[...] += matmul_t(grad_upper, up_ref[...])

    @pl.when(step == pl.num_programs(0) - 1)
    def _():
        grads = total_ref[...]
        normal = one_ref[...].astype(f32)
        grad_mixed = normalize_back(grads, normal, inv_one_ref[:, 0:1], gain_ref[0:1])
        attn = grad_mixed.astype(bf16)
        mixed_ref[...] = grad_mixed
        context_ref[...] = matmul_t(attn, out_w_ref[...]).astype(bf16)
        if keep:
            attn_ref[...] = attn
            sums_ref[0:1] = column_sum(grads * normal)
            sums_ref[2:3] = column_sum(attn.astype(f32))
            sums_ref[3:4] = column_sum(grads)


def before_attention(grads, stored, params, keep):
    attn, mlp, gains = params[:3]
    rows, width = grads.shape
    ff = stored["slope"].shape[1]
    tile = FF_TILE
    full = resident(rows, width)
    stat = resident(rows, PAIR)
    wide = pl.BlockSpec((rows, tile), lambda i: (0, i))
    full_type = jax.ShapeDtypeStruct((rows, width), bf16)
    specs = [full, full]
    types = [jax.ShapeDtypeStruct((rows, width), f32), full_type]
    if keep:
        specs += [full, full, wide, resident(8, width), pl.BlockSpec((1, tile), lambda i: (0, i))]
        types += [
            full_type,
            full_type,
            jax.ShapeDtypeStruct((rows, ff), bf16),
            jax.ShapeDtypeStruct((8, width), f32),
            jax.ShapeDtypeStruct((1, ff), f32),
        ]
    return pl.pallas_call(
        functools.partial(before_kernel, keep),
        grid=(ff // tile,),
        in_specs=[full, full, stat, wide, full, stat]
        + weight_specs(width, ff)
        + [resident(2, width)],
        out_specs=specs,
        out_shape=types,
        scratch_shapes=[pltpu.VMEM((rows, width), bf16), pltpu.VMEM((rows, width), f32)],
        cost_estimate=pl.CostEstimate(
            flops=2 * rows * width * (width + 2 * ff),
            bytes_accessed=2 * width * (width + 2 * ff) + 4 * rows * ff,
            transcendentals=0,
        ),
        name="before_attention",
    )(
        grads, stored["normal_two"], stored["inverse_two"], stored["slope"],
        stored["normal_one"], stored["inverse_one"], attn, mlp, mlp, gains,
    )


def project_back_kernel(mixed_ref, joint_ref, w_ref, out_ref):
    width = joint_ref.shape[2]
    total = mixed_ref[...]
    for place in range(3):
        total = total + matmul_t(joint_ref[place], w_ref[:, place * width : (place + 1) * width])
    out_ref[...] = total.astype(bf16)


def project_back(grad_mixed, grad_joint, whole):
    rows, width = grad_mixed.shape
    tile = 256
    return pl.pallas_call(
        project_back_kernel,
        grid=(width // tile,),
        in_specs=[
            pl.BlockSpec((rows, tile), lambda i: (0, i)),
            resident(3, rows, width),
            pl.BlockSpec((tile, 3 * width), lambda i: (i, 0)),
        ],
        out_specs=pl.BlockSpec((rows, tile), lambda i: (0, i)),
        out_shape=jax.ShapeDtypeStruct((rows, width), bf16),
        cost_estimate=pl.CostEstimate(
            flops=6 * rows * width * width,
            bytes_accessed=12 * rows * width + 6 * width * width,
            transcendentals=0,
        ),
        name="project_back",
    )(grad_mixed, grad_joint, whole)


def weight_grad_kernel(left_one, left_two, right_one, right_two, out_ref):
    total = tmatmul(left_one[...], right_one[...]) + tmatmul(left_two[...], right_two[...])
    out_ref[...] = total.astype(bf16)


def weight_grad(lefts, rights, tile_rows=512, tile_columns=1024):
    rows, height = lefts[0].shape
    stacked = rights[0].ndim == 3
    columns = rights[0].shape[-1]
    parts = rights[0].shape[0] if stacked else columns // tile_columns
    across = parts * columns // tile_columns if stacked else parts
    left = pl.BlockSpec((rows, tile_rows), lambda j, i: (0, i))
    if stacked:
        right = pl.BlockSpec((None, rows, tile_columns), lambda j, i: (j, 0, 0))
    else:
        right = pl.BlockSpec((rows, tile_columns), lambda j, i: (0, j))
    return pl.pallas_call(
        weight_grad_kernel,
        grid=(across, height // tile_rows),
        in_specs=[left, left, right, right],
        out_specs=pl.BlockSpec((tile_rows, tile_columns), lambda j, i: (i, j)),
        out_shape=jax.ShapeDtypeStruct((height, across * tile_columns), bf16),
        cost_estimate=pl.CostEstimate(
            flops=4 * rows * height * across * tile_columns,
            bytes_accessed=4 * rows * (height + across * tile_columns)
            + 2 * height * across * tile_columns,
            transcendentals=0,
        ),
        name="weight_grad",
    )(*lefts, *rights)


def attention(inputs, hot, bar, params):
    attn, shifts = params[0], params[3]
    bias = jnp.concatenate([shifts[0], jnp.zeros_like(shifts[0]), shifts[1]])[None]
    joint = project(inputs, attn, bias)
    return (joint,) + tuple(attend(joint, hot, bar))


def layer_forward(inputs, hot, bar, params):
    joint, context, total = attention(inputs, hot, bar, params)
    made = after_attention(inputs, context, params, True)
    names = (
        "hidden", "normal_one", "inverse_one", "activated", "slope", "normal_two", "inverse_two"
    )
    stored = dict(zip(names, made[1:]))
    stored.update(inputs=inputs, joint=joint, context=context, total=total)
    return made[0], stored


def layer_backward(grads, hot, bar, params, stored):
    made = before_attention(grads, stored, params, False)
    grad_joint, _ = attend_back(
        stored["joint"], hot, bar, stored["total"], stored["context"], made[1]
    )
    return project_back(made[0], grad_joint, params[0])


def spread_features(values, shards, reps):
    lead = values.shape[:-1]
    rows = values.shape[-1] // (shards * reps * FF_BLOCKS)
    split = values.reshape(lead + (shards, reps, FF_BLOCKS, rows))
    at = len(lead)
    order = tuple(range(at)) + (at + 2, at, at + 1, at + 3)
    return split.transpose(order).reshape(values.shape)


def restore_features(values, shards, reps):
    lead = values.shape[:-1]
    rows = values.shape[-1] // (shards * reps * FF_BLOCKS)
    split = values.reshape(lead + (FF_BLOCKS, shards, reps, rows))
    at = len(lead)
    order = tuple(range(at)) + (at + 1, at + 2, at, at + 3)
    return split.transpose(order).reshape(values.shape)


def half_of(values, rep, reps, axis=0):
    size = values.shape[axis] // reps
    return lax.dynamic_slice_in_dim(values, rep * size, size, axis)


def gather_params(w_qkv, w_out, w_up, w_down, norm_gains, biases, up_bias):
    shards, reps = lax.axis_size("shard"), lax.axis_size("rep")
    rep = lax.axis_index("rep")
    width = w_out.shape[1]
    rows = w_out.shape[0] // reps
    ff = w_up.shape[1]
    part = norm_gains.shape[1]
    down = half_of(w_down, rep, reps).reshape(FF_BLOCKS, rows, width)
    down = down.transpose(1, 0, 2).reshape(rows, FF_BLOCKS * width)
    small = jnp.concatenate([norm_gains, biases, up_bias.reshape(-1, part)])
    kinds = small.shape[0]
    small = half_of(small, rep, reps).reshape(-1)
    small = jnp.pad(small, (0, rows * PAIR - small.shape[0])).reshape(rows, PAIR)
    early = jnp.concatenate([half_of(w_qkv, rep, reps), half_of(w_out, rep, reps), small], axis=1)
    late = jnp.concatenate([spread_features(half_of(w_up, rep, reps), shards, reps), down], axis=1)
    if shards > LONGEST_RING:
        attn = lax.all_gather(early, ("shard", "rep"), axis=0, tiled=True)
        mlp = lax.all_gather(late, ("shard", "rep"), axis=0, tiled=True)
    else:
        attn, mlp = gather_rings(early, late)
    small = attn[:, 4 * width :].reshape(shards * reps, rows * PAIR)
    small = small[:, : kinds // reps * part].reshape(shards, kinds, part).astype(f32)
    gains = small[:, :2].transpose(1, 0, 2).reshape(2, width)
    shifts = small[:, 2:8].transpose(1, 0, 2).reshape(6, width)
    up_shift = spread_features(small[:, 8:].reshape(ff), shards, reps)
    return attn, mlp, gains, shifts, up_shift[None]


def ring_order(count):
    return list(range(0, count, 2)) + list(range(1, count, 2))[::-1]


def ring():
    shards, reps = lax.axis_size("shard"), lax.axis_size("rep")
    order = ring_order(shards)
    place = jnp.asarray([order.index(i) for i in range(shards)], jnp.int32)
    place = place[lax.axis_index("shard")]
    table = jnp.asarray(order, jnp.int32)
    route = []
    for i in range(shards):
        here, there = order[i], order[(i + 1) % shards]
        route.append((here * reps, there * reps))
        route.append((there * reps + 1, here * reps + 1))

    def behind(distance, rep):
        return table[(place - (1 - 2 * rep) * distance) % shards]

    return route, behind


def swapped(block):
    reps = lax.axis_size("rep")
    return lax.ppermute(block, "rep", [(i, (i + 1) % reps) for i in range(reps)])


LATE_START = 3


def gather_rings(early, late):
    shards, reps = lax.axis_size("shard"), lax.axis_size("rep")
    rep = lax.axis_index("rep")
    route, behind = ring()
    rows = early.shape[0]
    parts = [early, late]
    wholes = [jnp.zeros((shards * reps * rows, part.shape[1]), bf16) for part in parts]
    after = lax.optimization_barrier

    def put(which, step, block):
        other = swapped(block)
        for half, piece in ((rep, block), (1 - rep, other)):
            start = (behind(step, half) * reps + half) * rows
            wholes[which] = lax.dynamic_update_slice_in_dim(wholes[which], piece, start, 0)

    blocks = [early, late]
    for step in range(shards):
        put(0, step, blocks[0])
        if step == LATE_START:
            blocks[0], blocks[1] = after((blocks[0], blocks[1]))
        if step + 1 < shards:
            blocks[0] = lax.ppermute(blocks[0], ("shard", "rep"), route)
    for step in range(shards):
        put(1, step, blocks[1])
        if step + 1 < shards:
            blocks[1] = lax.ppermute(blocks[1], ("shard", "rep"), route)
    return wholes


def reduce_rows(terms, at=0):
    shards, rep = lax.axis_size("shard"), lax.axis_index("rep")
    pick = lambda values, place, axis: lax.dynamic_index_in_dim(values, place, axis, keepdims=False)
    own = pick(terms, rep, at + 1)
    other = swapped(pick(terms, 1 - rep, at + 1))
    if shards > LONGEST_RING:
        return lax.psum_scatter(own + other, "shard", scatter_dimension=at).astype(f32)
    route, behind = ring()
    arrived = None
    for step in range(shards):
        target = behind(1 + step, rep)
        total = pick(own, target, at).astype(f32) + pick(other, target, at).astype(f32)
        if arrived is not None:
            total = total + arrived.astype(f32)
        if step < shards - 1:
            arrived = lax.ppermute(total.astype(bf16), ("shard", "rep"), route)
    return total


def both_halves(half):
    rep = lax.axis_index("rep")
    other = swapped(half.astype(bf16)).astype(f32)
    return jnp.where(rep == 0, jnp.stack([half, other]), jnp.stack([other, half]))


def on_device(
    boundary_in, segment_ids, keep_mask, w_qkv, w_out, w_up, w_down, norm_gains, biases, up_bias
):
    shards, reps = lax.axis_size("shard"), lax.axis_size("rep")
    is_first = lax.axis_index("section") == 0
    tokens = boundary_in[0]
    width = tokens.shape[1]
    row_count = tokens.shape[0] // MICRO
    rows = w_out.shape[1] // reps
    params = gather_params(
        w_qkv[0], w_out[0], w_up[0], w_down[0], norm_gains[0], biases[0], up_bias[0]
    )
    codes = segment_ids * 2 + keep_mask
    lane = lax.broadcasted_iota(jnp.int32, (row_count, PAIR), 1) % HEAD
    masks = []
    for micro in range(MICRO):
        same = codes[micro][:, None] == lane
        hot = same.astype(bf16)
        bar = jnp.where(same | (lane >= CODES), 0.0, masked_score).astype(bf16)
        masks.append((hot, bar))
    own = [tokens[micro * row_count : (micro + 1) * row_count] for micro in range(MICRO)]

    after = lax.optimization_barrier

    contexts = [attention(own[micro], *masks[micro], params)[1] for micro in range(MICRO)]
    sent = []
    for micro in range(MICRO):
        middle = after_attention(own[micro], contexts[micro], params, False)[0]
        if micro + 1 < MICRO:
            middle, contexts[micro + 1] = after((middle, contexts[micro + 1]))
        else:
            middle, start = after((middle, own[0]))
        sent.append(lax.ppermute(middle, "section", [(0, 1)]))
    outputs, stash, sent_back = [], [], []
    starts = [start, own[1]]
    for micro in range(MICRO):
        inputs = jnp.where(is_first, starts[micro], sent[micro])
        result, stored = layer_forward(inputs, *masks[micro], params)
        result, grads = after((result, own[micro]))
        outputs.append(result)
        stash.append(stored)
        grads = layer_backward(grads, *masks[micro], params, stored)
        if micro + 1 < MICRO:
            grads, starts[micro + 1] = after((grads, starts[micro + 1]))
        else:
            grads, start = after((grads, own[0]))
        sent_back.append(lax.ppermute(grads, "section", [(1, 0)]))

    def grad_of(left, right):
        return weight_grad([stored[left] for stored in stash], [terms[right] for terms in used])

    made = []
    for micro in range(MICRO):
        grads = jnp.where(is_first, sent_back[micro], start if micro == 0 else own[micro])
        made.append(before_attention(grads, stash[micro], params, True))
    used = [dict(grad_attn=m[2], grad_branch=m[3], grad_upper=m[4]) for m in made]
    grad_down = grad_of("activated", "grad_branch")
    grad_down = grad_down.reshape(FF_BLOCKS, shards, reps, rows, width)
    grad_up = grad_of("hidden", "grad_upper").reshape(shards, reps, rows, -1)
    grad_out = grad_of("context", "grad_attn").reshape(shards, reps, rows, width)
    smalls = []
    for micro in range(MICRO):
        stored = stash[micro]
        grad_joint, sums = attend_back(
            stored["joint"], *masks[micro], stored["total"], stored["context"], made[micro][1]
        )
        used[micro]["grad_joint"] = grad_joint
        base = made[micro][5]
        smalls.append(
            jnp.concatenate(
                [base[:2], sums[0], sums[2], base[2:6], made[micro][6].reshape(-1, width)]
            )
        )
    smalls = sum(smalls[1:], smalls[0])
    grad_qkv = grad_of("inputs", "grad_joint").reshape(shards, reps, rows, 3 * width)
    grads_back = [
        project_back(made[micro][0], used[micro]["grad_joint"], params[0]) for micro in range(MICRO)
    ]
    part = width // shards
    small = jnp.concatenate(
        [
            smalls[:8].reshape(8, shards, part).transpose(1, 0, 2),
            restore_features(smalls[8:].reshape(-1), shards, reps).reshape(shards, -1, part),
        ],
        axis=1,
    )
    kinds = small.shape[1]
    small = small.reshape(shards, reps, -1)
    used_part = small.shape[2]
    small = jnp.pad(small, ((0, 0), (0, 0), (0, rows * PAIR - used_part)))
    small = small.reshape(shards, reps, rows, PAIR).astype(bf16)

    down_total = both_halves(reduce_rows(grad_down, 1))
    up_total = both_halves(restore_features(reduce_rows(grad_up), shards, reps))
    last_total = both_halves(
        reduce_rows(jnp.concatenate([grad_qkv, grad_out, small], axis=3))
    )
    small = last_total[:, :, 4 * width :].reshape(reps, -1)[:, :used_part]
    small = small.reshape(kinds, part)
    boundary_out = jnp.where(
        is_first, jnp.concatenate(grads_back, axis=0), jnp.concatenate(outputs, axis=0)
    )
    joined = lambda values: values.reshape((1, -1) + values.shape[2:])
    return (
        boundary_out[None],
        joined(last_total[:, :, : 3 * width]),
        joined(last_total[:, :, 3 * width : 4 * width]),
        joined(up_total),
        down_total.reshape(1, -1, width),
        small[:2][None],
        small[2:8][None],
        small[8:].reshape(1, -1),
    )


def solution(mesh):
    placed = (
        P("section", ("shard", "rep"), None),
        P(("shard", "rep"), None),
        P(("shard", "rep"), None),
        P("section", "shard", None),
        P("section", "shard", None),
        P("section", "shard", None),
        P("section", "shard", None),
        P("section", None, "shard"),
        P("section", None, "shard"),
        P("section", "shard"),
    )
    return jax.shard_map(
        on_device,
        mesh=mesh,
        in_specs=placed,
        out_specs=(
            P("section", ("shard", "rep"), None),
            P("section", "shard", None),
            P("section", "shard", None),
            P("section", "shard", None),
            P("section", "shard", None),
            P("section", None, "shard"),
            P("section", None, "shard"),
            P("section", "shard"),
        ),
        check_vma=False,
    )
```
